1024 devices in a mesh: ctx: 64 (over x_hi, z), fsdp: 16 (over x_lo, y, core).
Axes of the slice: x: 4 (x_hi: 2, x_lo: 2; x = x_hi * 2 + x_lo), y: 4, z: 32, core: 2. Of those that a mesh axis runs over, the one named last changes fastest.
Arguments:
- query_stream: bfloat16 [8192, 8192], P('ctx', 'fsdp'), may hold values from -6 to 6
- key_stream: bfloat16 [8192, 8192], P('ctx', 'fsdp'), may hold values from -6 to 6
- value_stream: bfloat16 [8192, 8192], P('ctx', 'fsdp'), may hold values from -6 to 6
- conv_weight: float32 [3, 3, 8192], P(None, None, 'fsdp'), may hold values from -3.5 to 3.5
- decay_rates: float32 [16, 8192], P(None, 'fsdp'), may hold values from 3.0517578e-05 to 0.05, as said below
- residues: float32 [16, 8192], P(None, 'fsdp'), may hold values from -0.31622777 to 0.31622777
- skip_gain: float32 [8192], P('fsdp'), may hold values from -4 to 4
Outputs:
- gated_output: bfloat16 [8192, 8192], P('ctx', 'fsdp')
The draws below stay inside these ranges and needn't reach their ends.
Inputs may be any that keep to these rules, and one draw needn't show every extreme that they name: `decay_rates`: all rates are positive.
All inputs are finite; a program needn't handle non-finite values.
Results may differ from the reference program's by a relative error of at most 0.0053.
Values may be sent and summed in bfloat16 or wider, within the bound.
A program may use at most 32 MiB of HBM per device.

```python
import math
import jax
import jax.numpy as jnp
from jax import lax

D = 8192
ORDER = 16
TOKENS = 8192


def rate_table(key):
    uniform_draw = jax.random.uniform(jax.random.fold_in(key, 11), (ORDER, D), jnp.float32)
    low_end = math.log(min(0.5 / TOKENS, 0.05))
    high_end = math.log(0.05)
    return jnp.exp(low_end + (high_end - low_end) * uniform_draw)


def draw_decay_rates(key, part):
    return rate_table(key)


def draw_residues(key, part):
    rate_values = rate_table(key)
    normal_draw = jax.random.truncated_normal(jax.random.fold_in(key, 23), -4.0, 4.0, (ORDER, D), jnp.float32)
    return normal_draw * jnp.sqrt(2.0 * rate_values / ORDER)


def block_scale(rng, shape, split, least, high):
    loudness, own = 1.0, jax.random.fold_in(rng, 6)
    for axis_at, parts in split:
        steps = jnp.exp(jax.random.uniform(jax.random.fold_in(own, axis_at), (parts,), jnp.float32, least / len(split), high / len(split)))
        loudness = loudness * jnp.repeat(steps, shape[axis_at] // parts).reshape([-1 if axis == axis_at else 1 for axis in range(len(shape))])
    return loudness


def normal_values(rng, extent, scale, most, shards=(), kind=jnp.bfloat16):
    values = scale * jax.random.normal(rng, extent, jnp.float32)
    if shards:
        values = values * block_scale(rng, extent, shards, -0.22, 0.18)
    return jnp.clip(values, -most, most).astype(kind)


def setup_inputs(seed: int = 0) -> dict:
    keys = jax.random.split(jax.random.key(seed), 8)
    return {
        "query_stream": normal_values(keys[0], (TOKENS, D), 1.0, 6.0, ((0, 64), (1, 16))),
        "key_stream": normal_values(keys[1], (TOKENS, D), 1.0, 6.0, ((0, 64), (1, 16))),
        "value_stream": normal_values(keys[2], (TOKENS, D), 1.0, 6.0, ((0, 64), (1, 16))),
        "conv_weight": normal_values(keys[3], (3, 3, D), 3 ** -0.5, 3.5, ((2, 16),), jnp.float32),
        "decay_rates": draw_decay_rates(jax.random.fold_in(keys[7], 71), 0),
        "residues": draw_residues(jax.random.fold_in(keys[7], 71), 0),
        "skip_gain": normal_values(keys[6], (D,), 1.0, 4.0, ((0, 16),), jnp.float32),
    }


def short_conv(stream, tap_weights):
    signal = stream.astype(jnp.float32)
    padded = jnp.concatenate([jnp.zeros((2, signal.shape[1]), jnp.float32), signal], axis=0)
    return tap_weights[0][None, :] * signal + tap_weights[1][None, :] * padded[1:-1] + tap_weights[2][None, :] * padded[:-2]


def reference(query_stream, key_stream, value_stream, conv_weight, decay_rates, residues, skip_gain):
    q_short = short_conv(query_stream, conv_weight[0])
    k_short = short_conv(key_stream, conv_weight[1])
    v_short = short_conv(value_stream, conv_weight[2])
    product = lax.optimization_barrier((k_short * v_short).astype(jnp.bfloat16))
    block_size = math.gcd(D, 512)
    block_count = D // block_size
    columns = product.T.reshape(block_count, block_size, TOKENS)
    rate_blocks = decay_rates.reshape(ORDER, block_count, block_size).transpose(1, 0, 2)
    residue_blocks = residues.reshape(ORDER, block_count, block_size).transpose(1, 0, 2)

    def filter_block(operands):
        channel_rows, rate_rows, residue_rows = operands
        positions = jnp.arange(TOKENS, dtype=jnp.float32)

        def add_pole(pole_index, running):
            return running + residue_rows[pole_index][:, None] * jnp.exp(-rate_rows[pole_index][:, None] * positions[None, :])

        kernel = lax.fori_loop(0, ORDER, add_pole, jnp.zeros((block_size, TOKENS), jnp.float32))
        spectrum = jnp.fft.rfft(channel_rows.astype(jnp.float32), n=2 * TOKENS, axis=1) * jnp.fft.rfft(kernel, n=2 * TOKENS, axis=1)
        return jnp.fft.irfft(spectrum, n=2 * TOKENS, axis=1)[:, :TOKENS].astype(jnp.bfloat16)

    long_part = lax.map(filter_block, (columns, rate_blocks, residue_blocks)).reshape(D, TOKENS).T
    long_part = lax.optimization_barrier(long_part)
    mixed_sum = long_part.astype(jnp.float32) + skip_gain[None, :] * product.astype(jnp.float32)
    return (q_short * mixed_sum).astype(jnp.bfloat16)
```

```python
import functools

import jax
import jax.numpy as jnp
from jax import lax
from jax.experimental import pallas as pl
from jax.experimental.pallas import tpu as pltpu
from jax.sharding import PartitionSpec as P

MESH = pl.DeviceIdType.MESH
F32 = jnp.float32
BF16 = jnp.bfloat16
SUB = 16
PAD = 8
MEMBERS = 4
LANES = 128


def kernel(
    z_len, groups,
    q_hbm, k_hbm, v_hbm, cw_ref, rate_ref, res_ref, skip_ref, out_ref,
    raw, padded, edge, halo, xs, qs, etab, hpad, htab, ylocal, prefix, carried,
    apow, tbuf, got1, gbuf, got2, cbuf, got3,
    in_sem, halo_send, halo_recv, send1, recv1, sendx, recvx, send2, recv2, send3, recv3,
):
    tokens, width = out_ref.shape
    subs = tokens // SUB
    quarters = width // LANES
    poles = rate_ref.shape[0]
    ctx = lax.axis_index("ctx")
    half, z = ctx // z_len, ctx % z_len
    group, member = z // MEMBERS, z % MEMBERS
    ctx_len = 2 * z_len

    def place(to_half, to_group, to_member):
        return {"ctx": to_half * z_len + to_group * MEMBERS + to_member}

    loads = []
    for i, ref in enumerate((k_hbm, v_hbm, q_hbm)):
        load = pltpu.make_async_copy(ref, raw.at[i], in_sem.at[i])
        load.start()
        loads.append(load)

    after = {"ctx": lax.rem(ctx + 1, ctx_len)}
    before = {"ctx": lax.rem(ctx + ctx_len - 1, ctx_len)}
    partners = [after, before]
    for o in range(1, MEMBERS):
        partners.append(place(half, group, (member + o) % MEMBERS))
    for o in range(MEMBERS):
        partners.append(place(1 - half, group, o))
    for o in range(1, groups):
        partners.append(place(half, (group + o) % groups, member))
    barrier = pltpu.get_barrier_semaphore()
    for partner in partners:
        pl.semaphore_signal(barrier, inc=1, device_id=partner, device_id_type=MESH)

    steps = lax.broadcasted_iota(jnp.int32, (SUB, width), 0).astype(F32)
    taps = jnp.zeros((SUB, width), F32)
    for n in range(poles):
        row = res_ref[n : n + 1, :] * jnp.exp(-rate_ref[n : n + 1, :] * steps)
        etab[n] = row
        taps = taps + row
    hpad[0:SUB, :] = jnp.zeros((SUB, width), F32)
    hpad[SUB:, :] = taps
    for l in range(quarters):
        rates = rate_ref[:, l * LANES : (l + 1) * LANES]
        for i, power in enumerate((1, 2, 3) + tuple(range(4, 4 * groups + 1, 4))):
            apow[i, l] = jnp.exp(-rates * float(power * tokens))

    for i in range(3):
        loads[i].wait()
        padded[i, PAD:, :] = raw[i].astype(F32)
        edge[2 * i : 2 * i + 2, :] = padded[i, PAD + tokens - 2 :, :]
    edge[6:8, :] = jnp.zeros((2, width), F32)

    pl.semaphore_wait(barrier, len(partners))
    halo_copy = pltpu.make_async_remote_copy(
        edge, halo, halo_send, halo_recv, device_id=after, device_id_type=MESH
    )
    halo_copy.start()

    def short(i, stream, lo, hi):
        return (
            cw_ref[stream, 0:1, :] * padded[i, PAD + lo : PAD + hi, :]
            + cw_ref[stream, 1:2, :] * padded[i, PAD + lo - 1 : PAD + hi - 1, :]
            + cw_ref[stream, 2:3, :] * padded[i, PAD + lo - 2 : PAD + hi - 2, :]
        )

    def filter_rows(lo, hi):
        product = short(0, 1, lo, hi) * short(1, 2, lo, hi)
        xs[lo:hi, :] = product.astype(BF16).astype(F32)
        qs[lo:hi, :] = short(2, 0, lo, hi)

    def inner_states(blocks):
        for l in range(quarters):
            lanes = slice(l * LANES, (l + 1) * LANES)
            decay = jnp.exp(-rate_ref[:, lanes])
            states = [jnp.zeros((poles, LANES), F32) for _ in blocks]
            for s in range(SUB):
                for i, b in enumerate(blocks):
                    t = b * SUB + s
                    states[i] = (states[i] + xs[t : t + 1, lanes]) * decay
            for i, b in enumerate(blocks):
                prefix[b, l] = states[i]

    for b in range(1, subs):
        filter_rows(b * SUB, (b + 1) * SUB)
    inner_states(range(1, subs))
    halo_copy.wait()
    for i in range(3):
        padded[i, PAD - 2 : PAD, :] = jnp.where(ctx > 0, halo[2 * i : 2 * i + 2, :], 0.0)
    filter_rows(0, SUB)
    inner_states([0])

    for l in range(quarters):
        decay = jnp.exp(-rate_ref[:, l * LANES : (l + 1) * LANES] * float(SUB))
        state = jnp.zeros((poles, LANES), F32)
        for b in range(subs):
            grown = prefix[b, l]
            prefix[b, l] = state
            state = state * decay + grown
        tbuf[l] = state

    copies1 = []
    for o in range(1, MEMBERS):
        to = (member + o) % MEMBERS
        copy = pltpu.make_async_remote_copy(
            tbuf.at[to], got1.at[1, member], send1.at[o], recv1.at[member],
            device_id=place(half, group, to), device_id_type=MESH,
        )
        copy.start()
        copies1.append(copy)

    @pl.when(half == 0)
    def _():
        for o in range(MEMBERS):
            pltpu.make_async_remote_copy(
                tbuf.at[o], got1.at[0, member], sendx.at[o], recvx.at[member],
                device_id=place(1, group, o), device_id_type=MESH,
            ).start()

    for s in range(SUB):
        htab[s] = hpad[SUB - s : 2 * SUB - s, :]

    got1[1, member] = tbuf[member]
    for o in range(1, MEMBERS):
        source = (member + o) % MEMBERS
        pltpu.make_async_remote_copy(
            tbuf.at[0], got1.at[1, source], send1.at[o], recv1.at[source],
            device_id=place(half, group, source), device_id_type=MESH,
        ).wait_recv()

    @pl.when(half == 1)
    def _():
        for o in range(MEMBERS):
            pltpu.make_async_remote_copy(
                tbuf.at[0], got1.at[0, o], sendx.at[o], recvx.at[o],
                device_id=place(0, group, o), device_id_type=MESH,
            ).wait_recv()

    @pl.when(half == 0)
    def _():
        for o in range(MEMBERS):
            got1[0, o] = jnp.zeros((poles, LANES), F32)

    def total(side):
        return (
            got1[side, 3] + apow[0, member] * got1[side, 2]
            + apow[1, member] * got1[side, 1] + apow[2, member] * got1[side, 0]
        )

    first_total = total(0)
    own_total = total(1)
    gbuf[0] = own_total + apow[2 + groups, member] * first_total
    gbuf[1] = first_total

    copies2 = []
    for o in sorted(range(1, groups), key=lambda o: -min(o, groups - o)):
        wraps = (group + o) // groups
        copy = pltpu.make_async_remote_copy(
            gbuf.at[wraps], got2.at[o], send2.at[o], recv2.at[o],
            device_id=place(half, (group + o) % groups, member), device_id_type=MESH,
        )
        copy.start()
        copies2.append(copy)

    for l in range(quarters):
        lanes = slice(l * LANES, (l + 1) * LANES)
        sums = [jnp.zeros((SUB, LANES), F32) for _ in range(subs)]
        for s in range(SUB):
            table = htab[s, :, lanes]
            for b in range(subs):
                t = b * SUB + s
                sums[b] = sums[b] + table * xs[t : t + 1, lanes]
        for n in range(poles):
            table = etab[n, :, lanes]
            for b in range(1, subs):
                sums[b] = sums[b] + table * prefix[b, l, n : n + 1, :]
        for b in range(subs):
            ylocal[b * SUB : (b + 1) * SUB, lanes] = sums[b]

    inside = got1[1, 0]
    inner = [jnp.zeros((poles, LANES), F32), inside]
    for o in range(1, MEMBERS - 1):
        inside = inside * apow[0, member] + got1[1, o]
        inner.append(inside)
    carry = apow[2 + groups - 1, member] * gbuf[1]
    for o in sorted(range(1, groups), key=lambda o: min(o, groups - o)):
        pltpu.make_async_remote_copy(
            gbuf.at[0], got2.at[o], send2.at[o], recv2.at[o],
            device_id=place(half, (group + o) % groups, member), device_id_type=MESH,
        ).wait_recv()
        carry = carry + (got2[o] if o == 1 else apow[2 + o - 1, member] * got2[o])
    cbuf[0] = carry
    for o in range(1, MEMBERS):
        cbuf[o] = apow[o - 1, member] * carry + inner[o]
    got3[member] = cbuf[member]
    for o in range(1, MEMBERS):
        to = (member + o) % MEMBERS
        pltpu.make_async_remote_copy(
            cbuf.at[to], got3.at[member], send3.at[o], recv3.at[member],
            device_id=place(half, group, to), device_id_type=MESH,
        ).start()
    for o in range(1, MEMBERS):
        source = (member + o) % MEMBERS
        pltpu.make_async_remote_copy(
            cbuf.at[0], got3.at[source], send3.at[o], recv3.at[source],
            device_id=place(half, group, source), device_id_type=MESH,
        ).wait_recv()

    for l in range(quarters):
        lanes = slice(l * LANES, (l + 1) * LANES)
        decay = jnp.exp(-rate_ref[:, lanes] * float(SUB))
        state = got3[l]
        for b in range(subs):
            carried[b, l] = state
            state = state * decay
        sums = [ylocal[b * SUB : (b + 1) * SUB, lanes] for b in range(subs)]
        for n in range(poles):
            table = etab[n, :, lanes]
            for b in range(subs):
                sums[b] = sums[b] + table * carried[b, l, n : n + 1, :]
        for b in range(subs):
            rows = slice(b * SUB, (b + 1) * SUB)
            mixed = sums[b].astype(BF16).astype(F32) + skip_ref[:, lanes] * xs[rows, lanes]
            out_ref[rows, lanes] = (qs[rows, lanes] * mixed).astype(BF16)

    for copy in copies1 + copies2:
        copy.wait_send()

    @pl.when(half == 0)
    def _():
        for o in range(MEMBERS):
            pltpu.make_async_remote_copy(
                tbuf.at[o], got1.at[0, member], sendx.at[o], recvx.at[member],
                device_id=place(1, group, o), device_id_type=MESH,
            ).wait_send()

    for o in range(1, MEMBERS):
        to = (member + o) % MEMBERS
        pltpu.make_async_remote_copy(
            cbuf.at[to], got3.at[member], send3.at[o], recv3.at[member],
            device_id=place(half, group, to), device_id_type=MESH,
        ).wait_send()


def per_device(
    query_stream, key_stream, value_stream, conv_weight, decay_rates, residues, skip_gain
):
    tokens, width = query_stream.shape
    poles = decay_rates.shape[0]
    z_len = lax.axis_size("ctx") // 2
    groups = z_len // MEMBERS
    quarters = width // LANES
    subs = tokens // SUB
    vmem = pltpu.VMEM
    state = (poles, LANES)
    dma = pltpu.SemaphoreType.DMA
    whole = pl.BlockSpec(memory_space=pltpu.VMEM)
    anywhere = pl.BlockSpec(memory_space=pl.ANY)
    return pl.pallas_call(
        functools.partial(kernel, z_len, groups),
        out_shape=jax.ShapeDtypeStruct((tokens, width), BF16),
        in_specs=[anywhere] * 3 + [whole] * 4,
        out_specs=whole,
        scratch_shapes=[
            vmem((3, tokens, width), BF16),
            vmem((3, PAD + tokens, width), F32),
            vmem((8, width), F32),
            vmem((8, width), F32),
            vmem((tokens, width), F32),
            vmem((tokens, width), F32),
            vmem((poles, SUB, width), F32),
            vmem((2 * SUB, width), F32),
            vmem((SUB, SUB, width), F32),
            vmem((tokens, width), F32),
            vmem((subs, quarters) + state, F32),
            vmem((subs, quarters) + state, F32),
            vmem((3 + groups, quarters) + state, F32),
            vmem((quarters,) + state, F32),
            vmem((2, MEMBERS) + state, F32),
            vmem((2,) + state, F32),
            vmem((groups,) + state, F32),
            vmem((MEMBERS,) + state, F32),
            vmem((quarters,) + state, F32),
            dma((3,)), dma, dma,
            dma((MEMBERS,)), dma((MEMBERS,)), dma((MEMBERS,)), dma((MEMBERS,)),
            dma((groups,)), dma((groups,)), dma((MEMBERS,)), dma((MEMBERS,)),
        ],
        compiler_params=pltpu.CompilerParams(
            collective_id=0, has_side_effects=True, vmem_limit_bytes=40 * 1024 * 1024
        ),
        name="modal_scan",
    )(query_stream, key_stream, value_stream, conv_weight, decay_rates, residues,
      skip_gain.reshape(1, width))


def solution(mesh):
    in_specs = (
        P("ctx", "fsdp"),
        P("ctx", "fsdp"),
        P("ctx", "fsdp"),
        P(None, None, "fsdp"),
        P(None, "fsdp"),
        P(None, "fsdp"),
        P("fsdp"),
    )
    return jax.shard_map(
        per_device, mesh=mesh, in_specs=in_specs, out_specs=P("ctx", "fsdp"), check_vma=False
    )
```

```python
import functools

import jax
import jax.numpy as jnp
from jax import lax
from jax.experimental import pallas as pl
from jax.experimental.pallas import tpu as pltpu
from jax.sharding import PartitionSpec as P

MESH = pl.DeviceIdType.MESH
F32 = jnp.float32
BF16 = jnp.bfloat16
SUB = 16
PAD = 8
MEMBERS = 4
LANES = 128


def kernel(
    z_len, groups,
    q_hbm, k_hbm, v_hbm, cw_hbm, rate_hbm, res_hbm, skip_hbm, out_ref,
    cw_ref, rate_ref, res_ref, skip_ref, raw, padded, edge, halo, xs, qs, etab, hpad, htab, ylocal, prefix, carried,
    apow, tbuf, got1, gbuf, got2, cbuf, got3,
    in_sem, known, halo_send, halo_recv, send1, recv1, sendx, recvx, send2, recv2, send3, recv3,
):
    tokens, width = out_ref.shape
    subs = tokens // SUB
    quarters = width // LANES
    poles = rate_ref.shape[0]
    ctx = lax.axis_index("ctx")
    half, z = ctx // z_len, ctx % z_len
    group, member = z // MEMBERS, z % MEMBERS
    ctx_len = 2 * z_len

    def place(to_half, to_group, to_member):
        return {"ctx": to_half * z_len + to_group * MEMBERS + to_member}

    loads = []
    for source, target in (
        (rate_hbm, rate_ref), (res_hbm, res_ref), (k_hbm, raw.at[0]), (v_hbm, raw.at[1]),
        (cw_hbm, cw_ref), (q_hbm, raw.at[2]), (skip_hbm, skip_ref),
    ):
        load = pltpu.make_async_copy(source, target, in_sem.at[len(loads)])
        load.start()
        loads.append(load)

    after = {"ctx": lax.rem(ctx + 1, ctx_len)}
    before = {"ctx": lax.rem(ctx + ctx_len - 1, ctx_len)}
    near = (1, 2, groups - 2, groups - 1)
    partners = [before]
    for o in range(1, MEMBERS):
        partners.append(place(half, group, (member + o) % MEMBERS))
    for o in near:
        partners.append(place(half, (group + o) % groups, member))
    barrier = pltpu.get_barrier_semaphore()
    for partner in partners:
        pl.semaphore_signal(barrier, inc=1, device_id=partner, device_id_type=MESH)

    @pl.when(half == 1)
    def _():
        for o in range(MEMBERS):
            pl.semaphore_signal(
                barrier, inc=1, device_id=place(0, group, o), device_id_type=MESH
            )

    loads[0].wait()
    loads[1].wait()

    steps = lax.broadcasted_iota(jnp.int32, (SUB, width), 0).astype(F32)
    taps = jnp.zeros((SUB, width), F32)
    for n in range(poles):
        row = res_ref[n : n + 1, :] * jnp.exp(-rate_ref[n : n + 1, :] * steps)
        etab[n] = row
        taps = taps + row
    hpad[0:SUB, :] = jnp.zeros((SUB, width), F32)
    hpad[SUB:, :] = taps
    for l in range(quarters):
        rates = rate_ref[:, l * LANES : (l + 1) * LANES]
        for i, power in enumerate((1, 2, 3) + tuple(range(4, 4 * groups + 1, 4))):
            apow[i, l] = jnp.exp(-rates * float(power * tokens))

    for load in loads[2:]:
        load.wait()
    for i in range(3):
        padded[i, PAD:, :] = raw[i].astype(F32)
        edge[2 * i : 2 * i + 2, :] = padded[i, PAD + tokens - 2 :, :]
    edge[6:8, :] = jnp.zeros((2, width), F32)

    pl.semaphore_wait(barrier, len(partners) + MEMBERS * (1 - half))
    for o in (2, groups - 2):
        pl.semaphore_signal(
            known, inc=1, device_id=place(half, (group + o) % groups, member),
            device_id_type=MESH,
        )
    halo_copy = pltpu.make_async_remote_copy(
        edge, halo, halo_send, halo_recv, device_id=after, device_id_type=MESH
    )
    halo_copy.start()

    def short(i, stream, lo, hi):
        return (
            cw_ref[stream, 0:1, :] * padded[i, PAD + lo : PAD + hi, :]
            + cw_ref[stream, 1:2, :] * padded[i, PAD + lo - 1 : PAD + hi - 1, :]
            + cw_ref[stream, 2:3, :] * padded[i, PAD + lo - 2 : PAD + hi - 2, :]
        )

    def filter_rows(lo, hi):
        product = short(0, 1, lo, hi) * short(1, 2, lo, hi)
        xs[lo:hi, :] = product.astype(BF16).astype(F32)
        qs[lo:hi, :] = short(2, 0, lo, hi)

    def inner_states(blocks):
        for l in range(quarters):
            lanes = slice(l * LANES, (l + 1) * LANES)
            decay = jnp.exp(-rate_ref[:, lanes])
            states = [jnp.zeros((poles, LANES), F32) for _ in blocks]
            for s in range(SUB):
                for i, b in enumerate(blocks):
                    t = b * SUB + s
                    states[i] = (states[i] + xs[t : t + 1, lanes]) * decay
            for i, b in enumerate(blocks):
                prefix[b, l] = states[i]

    for b in range(1, subs):
        filter_rows(b * SUB, (b + 1) * SUB)
    inner_states(range(1, subs))
    halo_copy.wait()
    for i in range(3):
        padded[i, PAD - 2 : PAD, :] = jnp.where(ctx > 0, halo[2 * i : 2 * i + 2, :], 0.0)
    filter_rows(0, SUB)
    inner_states([0])

    for l in range(quarters):
        decay = jnp.exp(-rate_ref[:, l * LANES : (l + 1) * LANES] * float(SUB))
        state = jnp.zeros((poles, LANES), F32)
        for b in range(subs):
            grown = prefix[b, l]
            prefix[b, l] = state
            state = state * decay + grown
        tbuf[l] = state

    copies1 = []
    for o in range(1, MEMBERS):
        to = (member + o) % MEMBERS
        copy = pltpu.make_async_remote_copy(
            tbuf.at[to], got1.at[1, member], send1.at[o], recv1.at[member],
            device_id=place(half, group, to), device_id_type=MESH,
        )
        copy.start()
        copies1.append(copy)

    @pl.when(half == 0)
    def _():
        for o in range(MEMBERS):
            pltpu.make_async_remote_copy(
                tbuf.at[o], got1.at[0, member], sendx.at[o], recvx.at[member],
                device_id=place(1, group, o), device_id_type=MESH,
            ).start()

    for s in range(SUB):
        htab[s] = hpad[SUB - s : 2 * SUB - s, :]

    got1[1, member] = tbuf[member]
    for o in range(1, MEMBERS):
        source = (member + o) % MEMBERS
        pltpu.make_async_remote_copy(
            tbuf.at[0], got1.at[1, source], send1.at[o], recv1.at[source],
            device_id=place(half, group, source), device_id_type=MESH,
        ).wait_recv()

    @pl.when(half == 1)
    def _():
        for o in range(MEMBERS):
            pltpu.make_async_remote_copy(
                tbuf.at[0], got1.at[0, o], sendx.at[o], recvx.at[o],
                device_id=place(0, group, o), device_id_type=MESH,
            ).wait_recv()

    @pl.when(half == 0)
    def _():
        for o in range(MEMBERS):
            got1[0, o] = jnp.zeros((poles, LANES), F32)

    def total(side):
        return (
            got1[side, 3] + apow[0, member] * got1[side, 2]
            + apow[1, member] * got1[side, 1] + apow[2, member] * got1[side, 0]
        )

    first_total = total(0)
    own_total = total(1)
    gbuf[0] = own_total + apow[2 + groups, member] * first_total
    gbuf[1] = first_total

    pl.semaphore_wait(known, 2)
    copies2 = []
    for o in sorted(range(1, groups), key=lambda o: -min(o, groups - o)):
        wraps = (group + o) // groups
        copy = pltpu.make_async_remote_copy(
            gbuf.at[wraps], got2.at[o], send2.at[o], recv2.at[o],
            device_id=place(half, (group + o) % groups, member), device_id_type=MESH,
        )
        copy.start()
        copies2.append(copy)

    for l in range(quarters):
        lanes = slice(l * LANES, (l + 1) * LANES)
        sums = [jnp.zeros((SUB, LANES), F32) for _ in range(subs)]
        for s in range(SUB):
            table = htab[s, :, lanes]
            for b in range(subs):
                t = b * SUB + s
                sums[b] = sums[b] + table * xs[t : t + 1, lanes]
        for n in range(poles):
            table = etab[n, :, lanes]
            for b in range(1, subs):
                sums[b] = sums[b] + table * prefix[b, l, n : n + 1, :]
        for b in range(subs):
            ylocal[b * SUB : (b + 1) * SUB, lanes] = sums[b]

    inside = got1[1, 0]
    inner = [jnp.zeros((poles, LANES), F32), inside]
    for o in range(1, MEMBERS - 1):
        inside = inside * apow[0, member] + got1[1, o]
        inner.append(inside)
    carry = apow[2 + groups - 1, member] * gbuf[1]
    for o in sorted(range(1, groups), key=lambda o: min(o, groups - o)):
        pltpu.make_async_remote_copy(
            gbuf.at[0], got2.at[o], send2.at[o], recv2.at[o],
            device_id=place(half, (group + o) % groups, member), device_id_type=MESH,
        ).wait_recv()
        carry = carry + (got2[o] if o == 1 else apow[2 + o - 1, member] * got2[o])
    cbuf[0] = carry
    for o in range(1, MEMBERS):
        cbuf[o] = apow[o - 1, member] * carry + inner[o]
    got3[member] = cbuf[member]
    for o in range(1, MEMBERS):
        to = (member + o) % MEMBERS
        pltpu.make_async_remote_copy(
            cbuf.at[to], got3.at[member], send3.at[o], recv3.at[member],
            device_id=place(half, group, to), device_id_type=MESH,
        ).start()
    for o in range(1, MEMBERS):
        source = (member + o) % MEMBERS
        pltpu.make_async_remote_copy(
            cbuf.at[0], got3.at[source], send3.at[o], recv3.at[source],
            device_id=place(half, group, source), device_id_type=MESH,
        ).wait_recv()

    for l in range(quarters):
        lanes = slice(l * LANES, (l + 1) * LANES)
        decay = jnp.exp(-rate_ref[:, lanes] * float(SUB))
        state = got3[l]
        for b in range(subs):
            carried[b, l] = state
            state = state * decay
        sums = [ylocal[b * SUB : (b + 1) * SUB, lanes] for b in range(subs)]
        for n in range(poles):
            table = etab[n, :, lanes]
            for b in range(subs):
                sums[b] = sums[b] + table * carried[b, l, n : n + 1, :]
        for b in range(subs):
            rows = slice(b * SUB, (b + 1) * SUB)
            mixed = sums[b].astype(BF16).astype(F32) + skip_ref[:, lanes] * xs[rows, lanes]
            out_ref[rows, lanes] = (qs[rows, lanes] * mixed).astype(BF16)

    for copy in copies1 + copies2:
        copy.wait_send()

    @pl.when(half == 0)
    def _():
        for o in range(MEMBERS):
            pltpu.make_async_remote_copy(
                tbuf.at[o], got1.at[0, member], sendx.at[o], recvx.at[member],
                device_id=place(1, group, o), device_id_type=MESH,
            ).wait_send()

    for o in range(1, MEMBERS):
        to = (member + o) % MEMBERS
        pltpu.make_async_remote_copy(
            cbuf.at[to], got3.at[member], send3.at[o], recv3.at[member],
            device_id=place(half, group, to), device_id_type=MESH,
        ).wait_send()


def per_device(
    query_stream, key_stream, value_stream, conv_weight, decay_rates, residues, skip_gain
):
    tokens, width = query_stream.shape
    poles = decay_rates.shape[0]
    z_len = lax.axis_size("ctx") // 2
    groups = z_len // MEMBERS
    quarters = width // LANES
    subs = tokens // SUB
    vmem = pltpu.VMEM
    state = (poles, LANES)
    dma = pltpu.SemaphoreType.DMA
    whole = pl.BlockSpec(memory_space=pltpu.VMEM)
    outside = pl.BlockSpec(memory_space=pltpu.HBM)
    return pl.pallas_call(
        functools.partial(kernel, z_len, groups),
        out_shape=jax.ShapeDtypeStruct((tokens, width), BF16),
        in_specs=[outside] * 7,
        out_specs=whole,
        scratch_shapes=[
            vmem((3, 3, width), F32),
            vmem((poles, width), F32),
            vmem((poles, width), F32),
            vmem((1, width), F32),
            vmem((3, tokens, width), BF16),
            vmem((3, PAD + tokens, width), F32),
            vmem((8, width), F32),
            vmem((8, width), F32),
            vmem((tokens, width), F32),
            vmem((tokens, width), F32),
            vmem((poles, SUB, width), F32),
            vmem((2 * SUB, width), F32),
            vmem((SUB, SUB, width), F32),
            vmem((tokens, width), F32),
            vmem((subs, quarters) + state, F32),
            vmem((subs, quarters) + state, F32),
            vmem((3 + groups, quarters) + state, F32),
            vmem((quarters,) + state, F32),
            vmem((2, MEMBERS) + state, F32),
            vmem((2,) + state, F32),
            vmem((groups,) + state, F32),
            vmem((MEMBERS,) + state, F32),
            vmem((quarters,) + state, F32),
            dma((7,)), pltpu.SemaphoreType.REGULAR, dma, dma,
            dma((MEMBERS,)), dma((MEMBERS,)), dma((MEMBERS,)), dma((MEMBERS,)),
            dma((groups,)), dma((groups,)), dma((MEMBERS,)), dma((MEMBERS,)),
        ],
        compiler_params=pltpu.CompilerParams(
            collective_id=0, has_side_effects=True, vmem_limit_bytes=67_043_328
        ),
        name="modal_scan",
    )(query_stream, key_stream, value_stream, conv_weight, decay_rates, residues,
      skip_gain.reshape(1, width))


def solution(mesh):
    in_specs = (
        P("ctx", "fsdp"),
        P("ctx", "fsdp"),
        P("ctx", "fsdp"),
        P(None, None, "fsdp"),
        P(None, "fsdp"),
        P(None, "fsdp"),
        P("fsdp"),
    )
    return jax.shard_map(
        per_device, mesh=mesh, in_specs=in_specs, out_specs=P("ctx", "fsdp"), check_vma=False
    )
```

```python
import functools

import jax
import jax.numpy as jnp
from jax import lax
from jax.experimental import pallas as pl
from jax.experimental.pallas import tpu as pltpu
from jax.sharding import PartitionSpec as P

MESH = pl.DeviceIdType.MESH
F32 = jnp.float32
BF16 = jnp.bfloat16
SUB = 16
PAD = 8
EDGE = 8
MEMBERS = 4
LANES = 128


def kernel(
    z_len, groups,
    q_hbm, k_hbm, v_hbm, cw_hbm, rate_hbm, res_hbm, skip_hbm, out_ref,
    cw_ref, rate_ref, res_ref, skip_ref, raw, padded, edge, halo, xs, qs, etab, hpad, htab, ylocal, prefix, carried,
    apow, taps_ref, dec_ref, tbuf, got1, prev, gbuf, got2, cbuf, got3,
    in_sem, known, halo_send, halo_recv, send1, recv1, sendx, recvx, sende, recve, sendf, recvf, send2, recv2, send3, recv3,
):
    tokens, width = out_ref.shape
    subs = tokens // SUB
    quarters = width // LANES
    poles = rate_ref.shape[0]
    ctx = lax.axis_index("ctx")
    half, z = ctx // z_len, ctx % z_len
    group, member = z // MEMBERS, z % MEMBERS
    ctx_len = 2 * z_len

    def place(to_half, to_group, to_member):
        return {"ctx": to_half * z_len + to_group * MEMBERS + to_member}

    loads = []
    for source, target in (
        (rate_hbm, rate_ref), (res_hbm, res_ref), (k_hbm, raw.at[0]), (v_hbm, raw.at[1]),
        (cw_hbm, cw_ref), (q_hbm, raw.at[2]), (skip_hbm, skip_ref),
    ):
        load = pltpu.make_async_copy(source, target, in_sem.at[len(loads)])
        load.start()
        loads.append(load)

    after = {"ctx": lax.rem(ctx + 1, ctx_len)}
    before = {"ctx": lax.rem(ctx + ctx_len - 1, ctx_len)}
    near = (1, 2, groups - 2, groups - 1)
    partners = [before]
    for o in range(1, MEMBERS):
        partners.append(place(half, group, (member + o) % MEMBERS))
    for o in near:
        partners.append(place(half, (group + o) % groups, member))
    barrier = pltpu.get_barrier_semaphore()
    for partner in partners:
        pl.semaphore_signal(barrier, inc=1, device_id=partner, device_id_type=MESH)

    @pl.when(half == 1)
    def _():
        for o in range(MEMBERS):
            pl.semaphore_signal(
                barrier, inc=1, device_id=place(0, group, o), device_id_type=MESH
            )

    last = member == MEMBERS - 1
    block = half * groups + group
    left, right = lax.rem(block + 2 * groups - 1, 2 * groups), lax.rem(block + 1, 2 * groups)

    @pl.when(block > 0)
    def _():
        pl.semaphore_signal(
            barrier, inc=1, device_id=place(left // groups, left % groups, MEMBERS - 1),
            device_id_type=MESH,
        )

    @pl.when((half == 1) & (group > 0))
    def _():
        pl.semaphore_signal(
            barrier, inc=1, device_id=place(0, left % groups, MEMBERS - 1),
            device_id_type=MESH,
        )

    for load in loads:
        load.wait()
    for i in range(2):
        padded[i, 0:PAD, :] = jnp.zeros((PAD, width), F32)
        padded[i, PAD:, :] = raw[i].astype(F32)

    def short(i, stream, lo, hi):
        return (
            cw_ref[stream, 0:1, :] * padded[i, PAD + lo : PAD + hi, :]
            + cw_ref[stream, 1:2, :] * padded[i, PAD + lo - 1 : PAD + hi - 1, :]
            + cw_ref[stream, 2:3, :] * padded[i, PAD + lo - 2 : PAD + hi - 2, :]
        )

    def products(lo, hi):
        product = short(0, 1, lo, hi) * short(1, 2, lo, hi)
        xs[lo:hi, :] = product.astype(BF16).astype(F32)

    def inner_states(blocks):
        for l in range(quarters):
            lanes = slice(l * LANES, (l + 1) * LANES)
            decay = jnp.exp(-rate_ref[:, lanes])
            states = [jnp.zeros((poles, LANES), F32) for _ in blocks]
            for s in range(SUB):
                for i, b in enumerate(blocks):
                    t = b * SUB + s
                    states[i] = (states[i] + xs[t : t + 1, lanes]) * decay
            for i, b in enumerate(blocks):
                prefix[b, l] = states[i]

    for b in range(subs):
        products(b * SUB, (b + 1) * SUB)
    xs[0:2, :] = jnp.zeros((2, width), F32)
    for l in range(quarters):
        lanes = slice(l * LANES, (l + 1) * LANES)
        for i in range(2):
            first = cw_ref[i + 1, 0:1, lanes] * padded[i, PAD : PAD + 2, lanes]
            tbuf[l, poles + 2 * i : poles + 2 * i + 2, :] = first
            second = cw_ref[i + 1, 1:2, lanes] * padded[i, PAD : PAD + 1, lanes]
            tbuf[l, poles + 2 * i + 1 : poles + 2 * i + 2, :] = first[1:2, :] + second
            tbuf[l, poles + 4 + 2 * i : poles + 6 + 2 * i, :] = padded[
                i, PAD + tokens - 2 : PAD + tokens, lanes
            ]
    inner_states(range(subs))
    for l in range(quarters):
        decay = jnp.exp(-rate_ref[:, l * LANES : (l + 1) * LANES] * float(SUB))
        dec_ref[l] = decay
        state = prefix[0, l]
        for b in range(1, subs):
            state = state * decay + prefix[b, l]
        tbuf[l, 0:poles, :] = state

    onward = MEMBERS * jnp.where(block < 2 * groups - 1, 1, 0)
    across = MEMBERS * jnp.where((half == 0) & (group < groups - 1), 1, 0)
    pl.semaphore_wait(
        barrier,
        MEMBERS + len(near) + MEMBERS * (1 - half) + jnp.where(last, onward + across, 0),
    )

    copies1 = []
    for o in range(1, MEMBERS):
        to = (member + o) % MEMBERS
        copy = pltpu.make_async_remote_copy(
            tbuf.at[to], got1.at[1, member], send1.at[o], recv1.at[member],
            device_id=place(half, group, to), device_id_type=MESH,
        )
        copy.start()
        copies1.append(copy)

    @pl.when(half == 0)
    def _():
        for o in range(MEMBERS):
            pltpu.make_async_remote_copy(
                tbuf.at[o], got1.at[0, member], sendx.at[o], recvx.at[member],
                device_id=place(1, group, o), device_id_type=MESH,
            ).start()

    edge_sends = []
    for o in range(MEMBERS):
        edge_sends.append((last & (block < 2 * groups - 1), pltpu.make_async_remote_copy(
            tbuf.at[o, pl.ds(poles, EDGE)], prev.at[1], sende.at[o], recve,
            device_id=place(right // groups, right % groups, o), device_id_type=MESH,
        )))
        edge_sends.append((last & (half == 0) & (group < groups - 1), pltpu.make_async_remote_copy(
            tbuf.at[o, pl.ds(poles, EDGE)], prev.at[0], sendf.at[o], recvf,
            device_id=place(1, right % groups, o), device_id_type=MESH,
        )))
    for due, copy in edge_sends:

        @pl.when(due)
        def _():
            copy.start()

    for o in (2, groups - 2):
        pl.semaphore_signal(
            known, inc=1, device_id=place(half, (group + o) % groups, member),
            device_id_type=MESH,
        )

    padded[2, PAD:, :] = raw[2].astype(F32)
    for i in range(3):
        edge[2 * i : 2 * i + 2, :] = padded[i, PAD + tokens - 2 :, :]
    edge[6:8, :] = jnp.zeros((2, width), F32)
    halo_copy = pltpu.make_async_remote_copy(
        edge, halo, halo_send, halo_recv, device_id=after, device_id_type=MESH
    )
    halo_copy.start()

    steps = lax.broadcasted_iota(jnp.int32, (SUB, width), 0).astype(F32)
    taps = jnp.zeros((SUB, width), F32)
    for n in range(poles):
        row = res_ref[n : n + 1, :] * jnp.exp(-rate_ref[n : n + 1, :] * steps)
        etab[n] = row
        taps = taps + row
    hpad[0:SUB, :] = jnp.zeros((SUB, width), F32)
    hpad[SUB:, :] = taps
    for l in range(quarters):
        rates = rate_ref[:, l * LANES : (l + 1) * LANES]
        for i, power in enumerate((1, 2, 3) + tuple(range(4, 4 * groups + 1, 4))):
            apow[i, l] = jnp.exp(-rates * float(power * tokens))

    for l in range(quarters):
        lanes = slice(l * LANES, (l + 1) * LANES)
        rates = rate_ref[:, lanes]
        apow[3 + groups, l] = jnp.exp(-rates * float(tokens - 1))
        for i in range(2):
            taps_ref[l, 2 * i : 2 * i + 2, :] = cw_ref[i + 1, 1:3, lanes]
    for s in range(SUB):
        htab[s] = hpad[SUB - s : 2 * SUB - s, :]

    got1[1, member] = tbuf[member]
    for o in range(1, MEMBERS):
        source = (member + o) % MEMBERS
        pltpu.make_async_remote_copy(
            tbuf.at[0], got1.at[1, source], send1.at[o], recv1.at[source],
            device_id=place(half, group, source), device_id_type=MESH,
        ).wait_recv()

    @pl.when(half == 1)
    def _():
        for o in range(MEMBERS):
            pltpu.make_async_remote_copy(
                tbuf.at[0], got1.at[0, o], sendx.at[o], recvx.at[o],
                device_id=place(0, group, o), device_id_type=MESH,
            ).wait_recv()

    @pl.when(half == 0)
    def _():
        for o in range(MEMBERS):
            got1[0, o] = jnp.zeros((poles + EDGE, LANES), F32)

    @pl.when(block > 0)
    def _():
        pltpu.make_async_remote_copy(
            tbuf.at[0, pl.ds(poles, EDGE)], prev.at[1], sende.at[0], recve,
            device_id=after, device_id_type=MESH,
        ).wait_recv()

    @pl.when(block == 0)
    def _():
        prev[1] = jnp.zeros((EDGE, LANES), F32)

    @pl.when((half == 1) & (group > 0))
    def _():
        pltpu.make_async_remote_copy(
            tbuf.at[0, pl.ds(poles, EDGE)], prev.at[0], sendf.at[0], recvf,
            device_id=after, device_id_type=MESH,
        ).wait_recv()

    @pl.when((half == 0) | (group == 0))
    def _():
        prev[0] = jnp.zeros((EDGE, LANES), F32)

    def whole_states(side):
        states = []
        for o in range(MEMBERS):
            own = got1[side, o, poles : poles + EDGE, :]
            ahead = got1[side, o - 1, poles : poles + EDGE, :] if o else prev[side]
            firsts, seconds = [], []
            for i in range(2):
                one = taps_ref[member, 2 * i : 2 * i + 1, :]
                two = taps_ref[member, 2 * i + 1 : 2 * i + 2, :]
                older, newer = ahead[4 + 2 * i : 5 + 2 * i, :], ahead[5 + 2 * i : 6 + 2 * i, :]
                firsts.append(own[2 * i : 2 * i + 1, :] + one * newer + two * older)
                seconds.append(own[2 * i + 1 : 2 * i + 2, :] + two * newer)
            first = (firsts[0] * firsts[1]).astype(BF16).astype(F32)
            second = (seconds[0] * seconds[1]).astype(BF16).astype(F32)
            states.append(
                got1[side, o, 0:poles, :] + apow[0, member] * first
                + apow[3 + groups, member] * second
            )
        return states

    def total(states):
        return (
            states[3] + apow[0, member] * states[2]
            + apow[1, member] * states[1] + apow[2, member] * states[0]
        )

    first_total = total(whole_states(0))
    own_states = whole_states(1)
    own_total = total(own_states)
    gbuf[0] = own_total + apow[2 + groups, member] * first_total
    gbuf[1] = first_total

    pl.semaphore_wait(known, 2)
    copies2 = []
    for o in sorted(range(1, groups), key=lambda o: -min(o, groups - o)):
        wraps = (group + o) // groups
        copy = pltpu.make_async_remote_copy(
            gbuf.at[wraps], got2.at[o], send2.at[o], recv2.at[o],
            device_id=place(half, (group + o) % groups, member), device_id_type=MESH,
        )
        copy.start()
        copies2.append(copy)

    halo_copy.wait()
    for i in range(3):
        padded[i, PAD - 2 : PAD, :] = jnp.where(ctx > 0, halo[2 * i : 2 * i + 2, :], 0.0)
    products(0, SUB)
    inner_states([0])
    for b in range(subs):
        qs[b * SUB : (b + 1) * SUB, :] = short(2, 0, b * SUB, (b + 1) * SUB)
    for l in range(quarters):
        state = jnp.zeros((poles, LANES), F32)
        for b in range(subs):
            grown = prefix[b, l]
            prefix[b, l] = state
            state = state * dec_ref[l] + grown
    for l in range(quarters):
        lanes = slice(l * LANES, (l + 1) * LANES)
        sums = [jnp.zeros((SUB, LANES), F32) for _ in range(subs)]
        for s in range(SUB):
            table = htab[s, :, lanes]
            for b in range(subs):
                t = b * SUB + s
                sums[b] = sums[b] + table * xs[t : t + 1, lanes]
        for n in range(poles):
            table = etab[n, :, lanes]
            for b in range(1, subs):
                sums[b] = sums[b] + table * prefix[b, l, n : n + 1, :]
        for b in range(subs):
            ylocal[b * SUB : (b + 1) * SUB, lanes] = sums[b]

    inside = own_states[0]
    inner = [jnp.zeros((poles, LANES), F32), inside]
    for o in range(1, MEMBERS - 1):
        inside = inside * apow[0, member] + own_states[o]
        inner.append(inside)
    for o in range(1, MEMBERS):
        cbuf[o] = inner[o]
    carry = apow[2 + groups - 1, member] * gbuf[1]
    for o in sorted(range(1, groups), key=lambda o: min(o, groups - o)):
        pltpu.make_async_remote_copy(
            gbuf.at[0], got2.at[o], send2.at[o], recv2.at[o],
            device_id=place(half, (group + o) % groups, member), device_id_type=MESH,
        ).wait_recv()
        carry = carry + (got2[o] if o == 1 else apow[2 + o - 1, member] * got2[o])
    cbuf[0] = carry
    for o in range(1, MEMBERS):
        cbuf[o] = apow[o - 1, member] * carry + cbuf[o]
    got3[member] = cbuf[member]
    for o in range(1, MEMBERS):
        to = (member + o) % MEMBERS
        pltpu.make_async_remote_copy(
            cbuf.at[to], got3.at[member], send3.at[o], recv3.at[member],
            device_id=place(half, group, to), device_id_type=MESH,
        ).start()
    for o in range(1, MEMBERS):
        source = (member + o) % MEMBERS
        pltpu.make_async_remote_copy(
            cbuf.at[0], got3.at[source], send3.at[o], recv3.at[source],
            device_id=place(half, group, source), device_id_type=MESH,
        ).wait_recv()

    for l in range(quarters):
        lanes = slice(l * LANES, (l + 1) * LANES)
        decay = dec_ref[l]
        state = got3[l]
        for b in range(subs):
            carried[b, l] = state
            state = state * decay
        sums = [ylocal[b * SUB : (b + 1) * SUB, lanes] for b in range(subs)]
        for n in range(poles):
            table = etab[n, :, lanes]
            for b in range(subs):
                sums[b] = sums[b] + table * carried[b, l, n : n + 1, :]
        for b in range(subs):
            rows = slice(b * SUB, (b + 1) * SUB)
            mixed = sums[b].astype(BF16).astype(F32) + skip_ref[:, lanes] * xs[rows, lanes]
            out_ref[rows, lanes] = (qs[rows, lanes] * mixed).astype(BF16)

    for copy in copies1 + copies2:
        copy.wait_send()
    for due, copy in edge_sends:

        @pl.when(due)
        def _():
            copy.wait_send()

    @pl.when(half == 0)
    def _():
        for o in range(MEMBERS):
            pltpu.make_async_remote_copy(
                tbuf.at[o], got1.at[0, member], sendx.at[o], recvx.at[member],
                device_id=place(1, group, o), device_id_type=MESH,
            ).wait_send()

    for o in range(1, MEMBERS):
        to = (member + o) % MEMBERS
        pltpu.make_async_remote_copy(
            cbuf.at[to], got3.at[member], send3.at[o], recv3.at[member],
            device_id=place(half, group, to), device_id_type=MESH,
        ).wait_send()


def per_device(
    query_stream, key_stream, value_stream, conv_weight, decay_rates, residues, skip_gain
):
    tokens, width = query_stream.shape
    poles = decay_rates.shape[0]
    z_len = lax.axis_size("ctx") // 2
    groups = z_len // MEMBERS
    quarters = width // LANES
    subs = tokens // SUB
    vmem = pltpu.VMEM
    state = (poles, LANES)
    message = (poles + EDGE, LANES)
    dma = pltpu.SemaphoreType.DMA
    whole = pl.BlockSpec(memory_space=pltpu.VMEM)
    outside = pl.BlockSpec(memory_space=pltpu.HBM)
    return pl.pallas_call(
        functools.partial(kernel, z_len, groups),
        out_shape=jax.ShapeDtypeStruct((tokens, width), BF16),
        in_specs=[outside] * 7,
        out_specs=whole,
        scratch_shapes=[
            vmem((3, 3, width), F32),
            vmem((poles, width), F32),
            vmem((poles, width), F32),
            vmem((1, width), F32),
            vmem((3, tokens, width), BF16),
            vmem((3, PAD + tokens, width), F32),
            vmem((8, width), F32),
            vmem((8, width), F32),
            vmem((tokens, width), F32),
            vmem((tokens, width), F32),
            vmem((poles, SUB, width), F32),
            vmem((2 * SUB, width), F32),
            vmem((SUB, SUB, width), F32),
            vmem((tokens, width), F32),
            vmem((subs, quarters) + state, F32),
            vmem((subs, quarters) + state, F32),
            vmem((4 + groups, quarters) + state, F32),
            vmem((quarters, 8, LANES), F32),
            vmem((quarters,) + state, F32),
            vmem((quarters,) + message, F32),
            vmem((2, MEMBERS) + message, F32),
            vmem((2, EDGE, LANES), F32),
            vmem((2,) + state, F32),
            vmem((groups,) + state, F32),
            vmem((MEMBERS,) + state, F32),
            vmem((quarters,) + state, F32),
            dma((7,)), pltpu.SemaphoreType.REGULAR, dma, dma,
            dma((MEMBERS,)), dma((MEMBERS,)), dma((MEMBERS,)), dma((MEMBERS,)),
            dma((MEMBERS,)), dma, dma((MEMBERS,)), dma,
            dma((groups,)), dma((groups,)), dma((MEMBERS,)), dma((MEMBERS,)),
        ],
        compiler_params=pltpu.CompilerParams(
            collective_id=0, has_side_effects=True, vmem_limit_bytes=67_043_328
        ),
        name="modal_scan",
    )(query_stream, key_stream, value_stream, conv_weight, decay_rates, residues,
      skip_gain.reshape(1, width))


def solution(mesh):
    in_specs = (
        P("ctx", "fsdp"),
        P("ctx", "fsdp"),
        P("ctx", "fsdp"),
        P(None, None, "fsdp"),
        P(None, "fsdp"),
        P(None, "fsdp"),
        P("fsdp"),
    )
    return jax.shard_map(
        per_device, mesh=mesh, in_specs=in_specs, out_specs=P("ctx", "fsdp"), check_vma=False
    )
```

```python
import functools

import jax
import jax.numpy as jnp
from jax import lax
from jax.experimental import pallas as pl
from jax.experimental.pallas import tpu as pltpu
from jax.sharding import PartitionSpec as P

MESH = pl.DeviceIdType.MESH
F32 = jnp.float32
BF16 = jnp.bfloat16
SUB = 16
PAD = 8
EDGE = 8
MEMBERS = 4
LANES = 128


def kernel(
    z_len, groups,
    q_hbm, k_hbm, v_hbm, cw_hbm, rate_hbm, res_hbm, skip_hbm, out_ref,
    cw_ref, rate_ref, res_ref, skip_ref, raw, padded, edge, halo, xs, qs, etab, hpad, htab, ylocal, prefix, carried,
    apow, taps_ref, dec_ref, tbuf, got1, prev, gbuf, got2, cbuf, got3,
    in_sem, known, halo_send, halo_recv, send1, recv1, sendx, recvx, sende, recve, sendf, recvf, send2, recv2, send3, recv3,
):
    tokens, width = out_ref.shape
    subs = tokens // SUB
    quarters = width // LANES
    poles = rate_ref.shape[0]
    ctx = lax.axis_index("ctx")
    half, z = ctx // z_len, ctx % z_len
    group, member = z // MEMBERS, z % MEMBERS
    ctx_len = 2 * z_len

    def place(to_half, to_group, to_member):
        return {"ctx": to_half * z_len + to_group * MEMBERS + to_member}

    loads = []
    for source, target in (
        (rate_hbm, rate_ref), (res_hbm, res_ref), (k_hbm, raw.at[0]), (v_hbm, raw.at[1]),
        (cw_hbm, cw_ref), (q_hbm, raw.at[2]), (skip_hbm, skip_ref),
    ):
        load = pltpu.make_async_copy(source, target, in_sem.at[len(loads)])
        load.start()
        loads.append(load)

    after = {"ctx": lax.rem(ctx + 1, ctx_len)}
    before = {"ctx": lax.rem(ctx + ctx_len - 1, ctx_len)}
    near = (1, 2, groups - 2, groups - 1)
    partners = [before]
    for o in range(1, MEMBERS):
        partners.append(place(half, group, (member + o) % MEMBERS))
    for o in near:
        partners.append(place(half, (group + o) % groups, member))
    barrier = pltpu.get_barrier_semaphore()
    for partner in partners:
        pl.semaphore_signal(barrier, inc=1, device_id=partner, device_id_type=MESH)

    @pl.when(half == 1)
    def _():
        for o in range(MEMBERS):
            pl.semaphore_signal(
                barrier, inc=1, device_id=place(0, group, o), device_id_type=MESH
            )

    last = member == MEMBERS - 1
    block = half * groups + group
    left, right = lax.rem(block + 2 * groups - 1, 2 * groups), lax.rem(block + 1, 2 * groups)

    @pl.when(block > 0)
    def _():
        pl.semaphore_signal(
            barrier, inc=1, device_id=place(left // groups, left % groups, MEMBERS - 1),
            device_id_type=MESH,
        )

    @pl.when((half == 1) & (group > 0))
    def _():
        pl.semaphore_signal(
            barrier, inc=1, device_id=place(0, left % groups, MEMBERS - 1),
            device_id_type=MESH,
        )

    for load in loads:
        load.wait()
    for i in range(2):
        padded[i, 0:PAD, :] = jnp.zeros((PAD, width), F32)
        padded[i, PAD:, :] = raw[i].astype(F32)

    def short(i, stream, lo, hi):
        return (
            cw_ref[stream, 0:1, :] * padded[i, PAD + lo : PAD + hi, :]
            + cw_ref[stream, 1:2, :] * padded[i, PAD + lo - 1 : PAD + hi - 1, :]
            + cw_ref[stream, 2:3, :] * padded[i, PAD + lo - 2 : PAD + hi - 2, :]
        )

    def products(lo, hi):
        product = short(0, 1, lo, hi) * short(1, 2, lo, hi)
        xs[lo:hi, :] = product.astype(BF16).astype(F32)

    def inner_states(blocks):
        for l in range(quarters):
            lanes = slice(l * LANES, (l + 1) * LANES)
            decay = jnp.exp(-rate_ref[:, lanes])
            states = [jnp.zeros((poles, LANES), F32) for _ in blocks]
            for s in range(SUB):
                for i, b in enumerate(blocks):
                    t = b * SUB + s
                    states[i] = (states[i] + xs[t : t + 1, lanes]) * decay
            for i, b in enumerate(blocks):
                prefix[b, l] = states[i]

    for b in range(subs):
        products(b * SUB, (b + 1) * SUB)
    xs[0:2, :] = jnp.zeros((2, width), F32)
    for l in range(quarters):
        lanes = slice(l * LANES, (l + 1) * LANES)
        for i in range(2):
            first = cw_ref[i + 1, 0:1, lanes] * padded[i, PAD : PAD + 2, lanes]
            tbuf[l, poles + 2 * i : poles + 2 * i + 2, :] = first
            second = cw_ref[i + 1, 1:2, lanes] * padded[i, PAD : PAD + 1, lanes]
            tbuf[l, poles + 2 * i + 1 : poles + 2 * i + 2, :] = first[1:2, :] + second
            tbuf[l, poles + 4 + 2 * i : poles + 6 + 2 * i, :] = padded[
                i, PAD + tokens - 2 : PAD + tokens, lanes
            ]
    inner_states(range(subs))
    for l in range(quarters):
        decay = jnp.exp(-rate_ref[:, l * LANES : (l + 1) * LANES] * float(SUB))
        dec_ref[l] = decay
        state = prefix[0, l]
        for b in range(1, subs):
            state = state * decay + prefix[b, l]
        tbuf[l, 0:poles, :] = state

    onward = MEMBERS * jnp.where(block < 2 * groups - 1, 1, 0)
    across = MEMBERS * jnp.where((half == 0) & (group < groups - 1), 1, 0)
    pl.semaphore_wait(
        barrier,
        MEMBERS + len(near) + MEMBERS * (1 - half) + jnp.where(last, onward + across, 0),
    )

    copies1 = []
    for o in range(1, MEMBERS):
        to = (member + o) % MEMBERS
        copy = pltpu.make_async_remote_copy(
            tbuf.at[to], got1.at[1, member], send1.at[o], recv1.at[member],
            device_id=place(half, group, to), device_id_type=MESH,
        )
        copy.start()
        copies1.append(copy)

    @pl.when(half == 0)
    def _():
        for o in range(MEMBERS):
            pltpu.make_async_remote_copy(
                tbuf.at[o], got1.at[0, member], sendx.at[o], recvx.at[member],
                device_id=place(1, group, o), device_id_type=MESH,
            ).start()

    edge_sends = []
    for o in range(MEMBERS):
        edge_sends.append((last & (block < 2 * groups - 1), pltpu.make_async_remote_copy(
            tbuf.at[o, pl.ds(poles, EDGE)], prev.at[1], sende.at[o], recve,
            device_id=place(right // groups, right % groups, o), device_id_type=MESH,
        )))
        edge_sends.append((last & (half == 0) & (group < groups - 1), pltpu.make_async_remote_copy(
            tbuf.at[o, pl.ds(poles, EDGE)], prev.at[0], sendf.at[o], recvf,
            device_id=place(1, right % groups, o), device_id_type=MESH,
        )))
    for due, copy in edge_sends:

        @pl.when(due)
        def _():
            copy.start()

    for o in (2, groups - 2):
        pl.semaphore_signal(
            known, inc=1, device_id=place(half, (group + o) % groups, member),
            device_id_type=MESH,
        )

    padded[2, PAD:, :] = raw[2].astype(F32)
    for i in range(3):
        edge[2 * i : 2 * i + 2, :] = padded[i, PAD + tokens - 2 :, :]
    edge[6:8, :] = jnp.zeros((2, width), F32)
    halo_copy = pltpu.make_async_remote_copy(
        edge, halo, halo_send, halo_recv, device_id=after, device_id_type=MESH
    )
    halo_copy.start()

    steps = lax.broadcasted_iota(jnp.int32, (SUB, width), 0).astype(F32)
    taps = jnp.zeros((SUB, width), F32)
    for n in range(poles):
        row = res_ref[n : n + 1, :] * jnp.exp(-rate_ref[n : n + 1, :] * steps)
        etab[n] = row
        taps = taps + row
    hpad[0:SUB, :] = jnp.zeros((SUB, width), F32)
    hpad[SUB:, :] = taps
    for l in range(quarters):
        rates = rate_ref[:, l * LANES : (l + 1) * LANES]
        for i, power in enumerate((1, 2, 3) + tuple(range(4, 4 * groups + 1, 4))):
            apow[i, l] = jnp.exp(-rates * float(power * tokens))

    for l in range(quarters):
        lanes = slice(l * LANES, (l + 1) * LANES)
        rates = rate_ref[:, lanes]
        apow[3 + groups, l] = jnp.exp(-rates * float(tokens - 1))
        for i in range(2):
            taps_ref[l, 2 * i : 2 * i + 2, :] = cw_ref[i + 1, 1:3, lanes]
    for s in range(SUB):
        htab[s] = hpad[SUB - s : 2 * SUB - s, :]

    got1[1, member] = tbuf[member]
    for o in range(1, MEMBERS):
        source = (member + o) % MEMBERS
        pltpu.make_async_remote_copy(
            tbuf.at[0], got1.at[1, source], send1.at[o], recv1.at[source],
            device_id=place(half, group, source), device_id_type=MESH,
        ).wait_recv()

    @pl.when(half == 1)
    def _():
        for o in range(MEMBERS):
            pltpu.make_async_remote_copy(
                tbuf.at[0], got1.at[0, o], sendx.at[o], recvx.at[o],
                device_id=place(0, group, o), device_id_type=MESH,
            ).wait_recv()

    @pl.when(half == 0)
    def _():
        for o in range(MEMBERS):
            got1[0, o] = jnp.zeros((poles + EDGE, LANES), F32)

    @pl.when(block > 0)
    def _():
        pltpu.make_async_remote_copy(
            tbuf.at[0, pl.ds(poles, EDGE)], prev.at[1], sende.at[0], recve,
            device_id=after, device_id_type=MESH,
        ).wait_recv()

    @pl.when(block == 0)
    def _():
        prev[1] = jnp.zeros((EDGE, LANES), F32)

    @pl.when((half == 1) & (group > 0))
    def _():
        pltpu.make_async_remote_copy(
            tbuf.at[0, pl.ds(poles, EDGE)], prev.at[0], sendf.at[0], recvf,
            device_id=after, device_id_type=MESH,
        ).wait_recv()

    @pl.when((half == 0) | (group == 0))
    def _():
        prev[0] = jnp.zeros((EDGE, LANES), F32)

    def whole_states(side):
        states = []
        for o in range(MEMBERS):
            own = got1[side, o, poles : poles + EDGE, :]
            ahead = got1[side, o - 1, poles : poles + EDGE, :] if o else prev[side]
            firsts, seconds = [], []
            for i in range(2):
                one = taps_ref[member, 2 * i : 2 * i + 1, :]
                two = taps_ref[member, 2 * i + 1 : 2 * i + 2, :]
                older, newer = ahead[4 + 2 * i : 5 + 2 * i, :], ahead[5 + 2 * i : 6 + 2 * i, :]
                firsts.append(own[2 * i : 2 * i + 1, :] + one * newer + two * older)
                seconds.append(own[2 * i + 1 : 2 * i + 2, :] + two * newer)
            first = (firsts[0] * firsts[1]).astype(BF16).astype(F32)
            second = (seconds[0] * seconds[1]).astype(BF16).astype(F32)
            states.append(
                got1[side, o, 0:poles, :] + apow[0, member] * first
                + apow[3 + groups, member] * second
            )
        return states

    def total(states):
        return (
            states[3] + apow[0, member] * states[2]
            + apow[1, member] * states[1] + apow[2, member] * states[0]
        )

    first_total = total(whole_states(0))
    own_states = whole_states(1)
    own_total = total(own_states)
    gbuf[0] = own_total + apow[2 + groups, member] * first_total
    gbuf[1] = first_total

    pl.semaphore_wait(known, 2)
    copies2 = []
    for o in sorted(range(1, groups), key=lambda o: -min(o, groups - o)):
        wraps = (group + o) // groups
        copy = pltpu.make_async_remote_copy(
            gbuf.at[wraps], got2.at[o], send2.at[o], recv2.at[o],
            device_id=place(half, (group + o) % groups, member), device_id_type=MESH,
        )
        copy.start()
        copies2.append(copy)

    halo_copy.wait()
    for i in range(3):
        padded[i, PAD - 2 : PAD, :] = jnp.where(ctx > 0, halo[2 * i : 2 * i + 2, :], 0.0)
    products(0, SUB)
    inner_states([0])
    for b in range(subs):
        qs[b * SUB : (b + 1) * SUB, :] = short(2, 0, b * SUB, (b + 1) * SUB)
    for l in range(quarters):
        state = jnp.zeros((poles, LANES), F32)
        for b in range(subs):
            grown = prefix[b, l]
            prefix[b, l] = state
            state = state * dec_ref[l] + grown
    for l in range(quarters):
        lanes = slice(l * LANES, (l + 1) * LANES)
        sums = [jnp.zeros((SUB, LANES), F32) for _ in range(subs)]
        for s in range(SUB):
            table = htab[s, :, lanes]
            for b in range(subs):
                t = b * SUB + s
                sums[b] = sums[b] + table * xs[t : t + 1, lanes]
        for n in range(poles):
            table = etab[n, :, lanes]
            for b in range(1, subs):
                sums[b] = sums[b] + table * prefix[b, l, n : n + 1, :]
        for b in range(subs):
            ylocal[b * SUB : (b + 1) * SUB, lanes] = sums[b]

    inside = own_states[0]
    inner = [jnp.zeros((poles, LANES), F32), inside]
    for o in range(1, MEMBERS - 1):
        inside = inside * apow[0, member] + own_states[o]
        inner.append(inside)
    for o in range(1, MEMBERS):
        cbuf[o] = inner[o]
    carry = apow[2 + groups - 1, member] * gbuf[1]
    for o in sorted(range(1, groups), key=lambda o: min(o, groups - o)):
        pltpu.make_async_remote_copy(
            gbuf.at[0], got2.at[o], send2.at[o], recv2.at[o],
            device_id=place(half, (group + o) % groups, member), device_id_type=MESH,
        ).wait_recv()
        carry = carry + (got2[o] if o == 1 else apow[2 + o - 1, member] * got2[o])
    cbuf[0] = carry
    for o in range(1, MEMBERS):
        cbuf[o] = apow[o - 1, member] * carry + cbuf[o]
    got3[member] = cbuf[member]
    for o in range(1, MEMBERS):
        to = (member + o) % MEMBERS
        pltpu.make_async_remote_copy(
            cbuf.at[to], got3.at[member], send3.at[o], recv3.at[member],
            device_id=place(half, group, to), device_id_type=MESH,
        ).start()
    for o in range(1, MEMBERS):
        source = (member + o) % MEMBERS
        pltpu.make_async_remote_copy(
            cbuf.at[0], got3.at[source], send3.at[o], recv3.at[source],
            device_id=place(half, group, source), device_id_type=MESH,
        ).wait_recv()

    for l in range(quarters):
        lanes = slice(l * LANES, (l + 1) * LANES)
        decay = dec_ref[l]
        state = got3[l]
        for b in range(subs):
            carried[b, l] = state
            state = state * decay
        sums = [ylocal[b * SUB : (b + 1) * SUB, lanes] for b in range(subs)]
        for n in range(poles):
            table = etab[n, :, lanes]
            for b in range(subs):
                sums[b] = sums[b] + table * carried[b, l, n : n + 1, :]
        for b in range(subs):
            rows = slice(b * SUB, (b + 1) * SUB)
            mixed = sums[b].astype(BF16).astype(F32) + skip_ref[:, lanes] * xs[rows, lanes]
            out_ref[rows, lanes] = (qs[rows, lanes] * mixed).astype(BF16)

    for copy in copies1 + copies2:
        copy.wait_send()
    for due, copy in edge_sends:

        @pl.when(due)
        def _():
            copy.wait_send()

    @pl.when(half == 0)
    def _():
        for o in range(MEMBERS):
            pltpu.make_async_remote_copy(
                tbuf.at[o], got1.at[0, member], sendx.at[o], recvx.at[member],
                device_id=place(1, group, o), device_id_type=MESH,
            ).wait_send()

    for o in range(1, MEMBERS):
        to = (member + o) % MEMBERS
        pltpu.make_async_remote_copy(
            cbuf.at[to], got3.at[member], send3.at[o], recv3.at[member],
            device_id=place(half, group, to), device_id_type=MESH,
        ).wait_send()


def per_device(
    query_stream, key_stream, value_stream, conv_weight, decay_rates, residues, skip_gain
):
    tokens, width = query_stream.shape
    poles = decay_rates.shape[0]
    z_len = lax.axis_size("ctx") // 2
    groups = z_len // MEMBERS
    quarters = width // LANES
    subs = tokens // SUB
    vmem = pltpu.VMEM
    state = (poles, LANES)
    message = (poles + EDGE, LANES)
    dma = pltpu.SemaphoreType.DMA
    whole = pl.BlockSpec(memory_space=pltpu.VMEM)
    outside = pl.BlockSpec(memory_space=pltpu.HBM)
    return pl.pallas_call(
        functools.partial(kernel, z_len, groups),
        out_shape=jax.ShapeDtypeStruct((tokens, width), BF16),
        in_specs=[outside] * 7,
        out_specs=whole,
        scratch_shapes=[
            vmem((3, 3, width), F32),
            vmem((poles, width), F32),
            vmem((poles, width), F32),
            vmem((1, width), F32),
            vmem((3, tokens, width), BF16),
            vmem((3, PAD + tokens, width), F32),
            vmem((8, width), F32),
            vmem((8, width), F32),
            vmem((tokens, width), F32),
            vmem((tokens, width), F32),
            vmem((poles, SUB, width), F32),
            vmem((2 * SUB, width), F32),
            vmem((SUB, SUB, width), F32),
            vmem((tokens, width), F32),
            vmem((subs, quarters) + state, F32),
            vmem((subs, quarters) + state, F32),
            vmem((4 + groups, quarters) + state, F32),
            vmem((quarters, 8, LANES), F32),
            vmem((quarters,) + state, F32),
            vmem((quarters,) + message, F32),
            vmem((2, MEMBERS) + message, F32),
            vmem((2, EDGE, LANES), F32),
            vmem((2,) + state, F32),
            vmem((groups,) + state, F32),
            vmem((MEMBERS,) + state, F32),
            vmem((quarters,) + state, F32),
            dma((7,)), pltpu.SemaphoreType.REGULAR, dma, dma,
            dma((MEMBERS,)), dma((MEMBERS,)), dma((MEMBERS,)), dma((MEMBERS,)),
            dma((MEMBERS,)), dma, dma((MEMBERS,)), dma,
            dma((groups,)), dma((groups,)), dma((MEMBERS,)), dma((MEMBERS,)),
        ],
        compiler_params=pltpu.CompilerParams(
            collective_id=0, has_side_effects=True, vmem_limit_bytes=40 * 1024 * 1024
        ),
        name="modal_scan",
    )(*[
        pltpu.with_memory_space_constraint(operand, pltpu.HBM)
        for operand in (query_stream, key_stream, value_stream, conv_weight, decay_rates,
                        residues, skip_gain.reshape(1, width))
    ])


def solution(mesh):
    in_specs = (
        P("ctx", "fsdp"),
        P("ctx", "fsdp"),
        P("ctx", "fsdp"),
        P(None, None, "fsdp"),
        P(None, "fsdp"),
        P(None, "fsdp"),
        P("fsdp"),
    )
    return jax.shard_map(
        per_device, mesh=mesh, in_specs=in_specs, out_specs=P("ctx", "fsdp"), check_vma=False
    )
```

```python
import functools

import jax
import jax.numpy as jnp
from jax import lax
from jax.experimental import pallas as pl
from jax.experimental.pallas import tpu as pltpu
from jax.sharding import PartitionSpec as P

MESH = pl.DeviceIdType.MESH
F32 = jnp.float32
BF16 = jnp.bfloat16
SUB = 16
PAD = 8
EDGE = 8
MEMBERS = 4
LANES = 128


def kernel(
    z_len, groups,
    q_hbm, k_hbm, v_hbm, cw_hbm, rate_hbm, res_hbm, skip_hbm, out_ref,
    cw_ref, rate_ref, res_ref, skip_ref, raw, padded, edge, halo, xs, qs, etab, hpad, htab, ylocal, prefix, carried,
    apow, taps_ref, dec_ref, tbuf, got1, prev, gbuf, got2, cbuf, got3,
    in_sem, known, halo_send, halo_recv, send1, recv1, sendx, recvx, sende, recve, sendf, recvf, send2, recv2, send3, recv3,
):
    tokens, width = out_ref.shape
    subs = tokens // SUB
    quarters = width // LANES
    poles = rate_ref.shape[0]
    ctx = lax.axis_index("ctx")
    half, z = ctx // z_len, ctx % z_len
    group, member = z // MEMBERS, z % MEMBERS
    ctx_len = 2 * z_len

    def place(to_half, to_group, to_member):
        return {"ctx": to_half * z_len + to_group * MEMBERS + to_member}

    loads = []
    for source, target in (
        (rate_hbm, rate_ref), (res_hbm, res_ref), (k_hbm, raw.at[0]), (v_hbm, raw.at[1]),
        (cw_hbm, cw_ref), (q_hbm, raw.at[2]), (skip_hbm, skip_ref),
    ):
        load = pltpu.make_async_copy(source, target, in_sem.at[len(loads)])
        load.start()
        loads.append(load)

    after = {"ctx": lax.rem(ctx + 1, ctx_len)}
    before = {"ctx": lax.rem(ctx + ctx_len - 1, ctx_len)}
    near = (1, 2, groups - 2, groups - 1)
    partners = [before]
    for o in range(1, MEMBERS):
        partners.append(place(half, group, (member + o) % MEMBERS))
    for o in near:
        partners.append(place(half, (group + o) % groups, member))
    barrier = pltpu.get_barrier_semaphore()
    for partner in partners:
        pl.semaphore_signal(barrier, inc=1, device_id=partner, device_id_type=MESH)

    @pl.when(half == 1)
    def _():
        for o in range(MEMBERS):
            pl.semaphore_signal(
                barrier, inc=1, device_id=place(0, group, o), device_id_type=MESH
            )

    last = member == MEMBERS - 1
    block = half * groups + group
    left, right = lax.rem(block + 2 * groups - 1, 2 * groups), lax.rem(block + 1, 2 * groups)

    @pl.when(block > 0)
    def _():
        pl.semaphore_signal(
            barrier, inc=1, device_id=place(left // groups, left % groups, MEMBERS - 1),
            device_id_type=MESH,
        )

    @pl.when((half == 1) & (group > 0))
    def _():
        pl.semaphore_signal(
            barrier, inc=1, device_id=place(0, left % groups, MEMBERS - 1),
            device_id_type=MESH,
        )

    for load in loads:
        load.wait()
    for i in range(2):
        padded[i, 0:PAD, :] = jnp.zeros((PAD, width), F32)
        padded[i, PAD:, :] = raw[i].astype(F32)

    def short(i, stream, lo, hi):
        return (
            cw_ref[stream, 0:1, :] * padded[i, PAD + lo : PAD + hi, :]
            + cw_ref[stream, 1:2, :] * padded[i, PAD + lo - 1 : PAD + hi - 1, :]
            + cw_ref[stream, 2:3, :] * padded[i, PAD + lo - 2 : PAD + hi - 2, :]
        )

    def products(lo, hi):
        product = short(0, 1, lo, hi) * short(1, 2, lo, hi)
        xs[lo:hi, :] = product.astype(BF16).astype(F32)

    def inner_states(blocks):
        for l in range(quarters):
            lanes = slice(l * LANES, (l + 1) * LANES)
            decay = jnp.exp(-rate_ref[:, lanes])
            states = [jnp.zeros((poles, LANES), F32) for _ in blocks]
            for s in range(SUB):
                for i, b in enumerate(blocks):
                    t = b * SUB + s
                    states[i] = (states[i] + xs[t : t + 1, lanes]) * decay
            for i, b in enumerate(blocks):
                prefix[b, l] = states[i]

    for b in range(subs):
        products(b * SUB, (b + 1) * SUB)
    xs[0:2, :] = jnp.zeros((2, width), F32)
    for l in range(quarters):
        lanes = slice(l * LANES, (l + 1) * LANES)
        for i in range(2):
            first = cw_ref[i + 1, 0:1, lanes] * padded[i, PAD : PAD + 2, lanes]
            tbuf[l, poles + 2 * i : poles + 2 * i + 2, :] = first
            second = cw_ref[i + 1, 1:2, lanes] * padded[i, PAD : PAD + 1, lanes]
            tbuf[l, poles + 2 * i + 1 : poles + 2 * i + 2, :] = first[1:2, :] + second
            tbuf[l, poles + 4 + 2 * i : poles + 6 + 2 * i, :] = padded[
                i, PAD + tokens - 2 : PAD + tokens, lanes
            ]
    inner_states(range(subs))
    for l in range(quarters):
        decay = jnp.exp(-rate_ref[:, l * LANES : (l + 1) * LANES] * float(SUB))
        dec_ref[l] = decay
        state = prefix[0, l]
        for b in range(1, subs):
            state = state * decay + prefix[b, l]
        tbuf[l, 0:poles, :] = state

    onward = MEMBERS * jnp.where(block < 2 * groups - 1, 1, 0)
    across = MEMBERS * jnp.where((half == 0) & (group < groups - 1), 1, 0)
    pl.semaphore_wait(
        barrier,
        MEMBERS + len(near) + MEMBERS * (1 - half) + jnp.where(last, onward + across, 0),
    )

    copies1 = []
    for o in range(1, MEMBERS):
        to = (member + o) % MEMBERS
        copy = pltpu.make_async_remote_copy(
            tbuf.at[to], got1.at[1, member], send1.at[o], recv1.at[member],
            device_id=place(half, group, to), device_id_type=MESH,
        )
        copy.start()
        copies1.append(copy)

    @pl.when(half == 0)
    def _():
        for o in range(MEMBERS):
            pltpu.make_async_remote_copy(
                tbuf.at[o], got1.at[0, member], sendx.at[o], recvx.at[member],
                device_id=place(1, group, o), device_id_type=MESH,
            ).start()

    edge_sends = []
    for o in range(MEMBERS):
        edge_sends.append((last & (block < 2 * groups - 1), pltpu.make_async_remote_copy(
            tbuf.at[o, pl.ds(poles, EDGE)], prev.at[1], sende.at[o], recve,
            device_id=place(right // groups, right % groups, o), device_id_type=MESH,
        )))
        edge_sends.append((last & (half == 0) & (group < groups - 1), pltpu.make_async_remote_copy(
            tbuf.at[o, pl.ds(poles, EDGE)], prev.at[0], sendf.at[o], recvf,
            device_id=place(1, right % groups, o), device_id_type=MESH,
        )))
    for due, copy in edge_sends:

        @pl.when(due)
        def _():
            copy.start()

    for o in (2, groups - 2):
        pl.semaphore_signal(
            known, inc=1, device_id=place(half, (group + o) % groups, member),
            device_id_type=MESH,
        )

    padded[2, PAD:, :] = raw[2].astype(F32)
    for i in range(3):
        edge[2 * i : 2 * i + 2, :] = padded[i, PAD + tokens - 2 :, :]
    edge[6:8, :] = jnp.zeros((2, width), F32)
    halo_copy = pltpu.make_async_remote_copy(
        edge, halo, halo_send, halo_recv, device_id=after, device_id_type=MESH
    )
    halo_copy.start()

    for l in range(quarters):
        rates = rate_ref[:, l * LANES : (l + 1) * LANES]
        for i, power in enumerate((1, 2, 3) + tuple(range(4, 4 * groups + 1, 4))):
            apow[i, l] = jnp.exp(-rates * float(power * tokens))

    for l in range(quarters):
        lanes = slice(l * LANES, (l + 1) * LANES)
        rates = rate_ref[:, lanes]
        apow[3 + groups, l] = jnp.exp(-rates * float(tokens - 1))
        for i in range(2):
            taps_ref[l, 2 * i : 2 * i + 2, :] = cw_ref[i + 1, 1:3, lanes]

    got1[1, member] = tbuf[member]
    for o in range(1, MEMBERS):
        source = (member + o) % MEMBERS
        pltpu.make_async_remote_copy(
            tbuf.at[0], got1.at[1, source], send1.at[o], recv1.at[source],
            device_id=place(half, group, source), device_id_type=MESH,
        ).wait_recv()

    @pl.when(half == 1)
    def _():
        for o in range(MEMBERS):
            pltpu.make_async_remote_copy(
                tbuf.at[0], got1.at[0, o], sendx.at[o], recvx.at[o],
                device_id=place(0, group, o), device_id_type=MESH,
            ).wait_recv()

    @pl.when(half == 0)
    def _():
        for o in range(MEMBERS):
            got1[0, o] = jnp.zeros((poles + EDGE, LANES), F32)

    @pl.when(block > 0)
    def _():
        pltpu.make_async_remote_copy(
            tbuf.at[0, pl.ds(poles, EDGE)], prev.at[1], sende.at[0], recve,
            device_id=after, device_id_type=MESH,
        ).wait_recv()

    @pl.when(block == 0)
    def _():
        prev[1] = jnp.zeros((EDGE, LANES), F32)

    @pl.when((half == 1) & (group > 0))
    def _():
        pltpu.make_async_remote_copy(
            tbuf.at[0, pl.ds(poles, EDGE)], prev.at[0], sendf.at[0], recvf,
            device_id=after, device_id_type=MESH,
        ).wait_recv()

    @pl.when((half == 0) | (group == 0))
    def _():
        prev[0] = jnp.zeros((EDGE, LANES), F32)

    def whole_states(side):
        states = []
        for o in range(MEMBERS):
            own = got1[side, o, poles : poles + EDGE, :]
            ahead = got1[side, o - 1, poles : poles + EDGE, :] if o else prev[side]
            firsts, seconds = [], []
            for i in range(2):
                one = taps_ref[member, 2 * i : 2 * i + 1, :]
                two = taps_ref[member, 2 * i + 1 : 2 * i + 2, :]
                older, newer = ahead[4 + 2 * i : 5 + 2 * i, :], ahead[5 + 2 * i : 6 + 2 * i, :]
                firsts.append(own[2 * i : 2 * i + 1, :] + one * newer + two * older)
                seconds.append(own[2 * i + 1 : 2 * i + 2, :] + two * newer)
            first = (firsts[0] * firsts[1]).astype(BF16).astype(F32)
            second = (seconds[0] * seconds[1]).astype(BF16).astype(F32)
            states.append(
                got1[side, o, 0:poles, :] + apow[0, member] * first
                + apow[3 + groups, member] * second
            )
        return states

    def total(states):
        return (
            states[3] + apow[0, member] * states[2]
            + apow[1, member] * states[1] + apow[2, member] * states[0]
        )

    first_total = total(whole_states(0))
    own_states = whole_states(1)
    own_total = total(own_states)
    gbuf[0] = own_total + apow[2 + groups, member] * first_total
    gbuf[1] = first_total

    pl.semaphore_wait(known, 2)
    copies2 = []
    for o in sorted(range(1, groups), key=lambda o: -min(o, groups - o)):
        wraps = (group + o) // groups
        copy = pltpu.make_async_remote_copy(
            gbuf.at[wraps], got2.at[o], send2.at[o], recv2.at[o],
            device_id=place(half, (group + o) % groups, member), device_id_type=MESH,
        )
        copy.start()
        copies2.append(copy)

    steps = lax.broadcasted_iota(jnp.int32, (SUB, width), 0).astype(F32)
    taps = jnp.zeros((SUB, width), F32)
    for n in range(poles):
        row = res_ref[n : n + 1, :] * jnp.exp(-rate_ref[n : n + 1, :] * steps)
        etab[n] = row
        taps = taps + row
    hpad[0:SUB, :] = jnp.zeros((SUB, width), F32)
    hpad[SUB:, :] = taps
    for s in range(SUB):
        htab[s] = hpad[SUB - s : 2 * SUB - s, :]

    halo_copy.wait()
    for i in range(3):
        padded[i, PAD - 2 : PAD, :] = jnp.where(ctx > 0, halo[2 * i : 2 * i + 2, :], 0.0)
    products(0, SUB)
    inner_states([0])
    for b in range(subs):
        qs[b * SUB : (b + 1) * SUB, :] = short(2, 0, b * SUB, (b + 1) * SUB)
    for l in range(quarters):
        state = jnp.zeros((poles, LANES), F32)
        for b in range(subs):
            grown = prefix[b, l]
            prefix[b, l] = state
            state = state * dec_ref[l] + grown
    for l in range(quarters):
        lanes = slice(l * LANES, (l + 1) * LANES)
        sums = [jnp.zeros((SUB, LANES), F32) for _ in range(subs)]
        for s in range(SUB):
            table = htab[s, :, lanes]
            for b in range(subs):
                t = b * SUB + s
                sums[b] = sums[b] + table * xs[t : t + 1, lanes]
        for n in range(poles):
            table = etab[n, :, lanes]
            for b in range(1, subs):
                sums[b] = sums[b] + table * prefix[b, l, n : n + 1, :]
        for b in range(subs):
            ylocal[b * SUB : (b + 1) * SUB, lanes] = sums[b]

    inside = own_states[0]
    inner = [jnp.zeros((poles, LANES), F32), inside]
    for o in range(1, MEMBERS - 1):
        inside = inside * apow[0, member] + own_states[o]
        inner.append(inside)
    for o in range(1, MEMBERS):
        cbuf[o] = inner[o]
    carry = apow[2 + groups - 1, member] * gbuf[1]
    for o in sorted(range(1, groups), key=lambda o: min(o, groups - o)):
        pltpu.make_async_remote_copy(
            gbuf.at[0], got2.at[o], send2.at[o], recv2.at[o],
            device_id=place(half, (group + o) % groups, member), device_id_type=MESH,
        ).wait_recv()
        carry = carry + (got2[o] if o == 1 else apow[2 + o - 1, member] * got2[o])
    cbuf[0] = carry
    for o in range(1, MEMBERS):
        cbuf[o] = apow[o - 1, member] * carry + cbuf[o]
    got3[member] = cbuf[member]
    for o in range(1, MEMBERS):
        to = (member + o) % MEMBERS
        pltpu.make_async_remote_copy(
            cbuf.at[to], got3.at[member], send3.at[o], recv3.at[member],
            device_id=place(half, group, to), device_id_type=MESH,
        ).start()
    for o in range(1, MEMBERS):
        source = (member + o) % MEMBERS
        pltpu.make_async_remote_copy(
            cbuf.at[0], got3.at[source], send3.at[o], recv3.at[source],
            device_id=place(half, group, source), device_id_type=MESH,
        ).wait_recv()

    for l in range(quarters):
        lanes = slice(l * LANES, (l + 1) * LANES)
        decay = dec_ref[l]
        state = got3[l]
        for b in range(subs):
            carried[b, l] = state
            state = state * decay
        sums = [ylocal[b * SUB : (b + 1) * SUB, lanes] for b in range(subs)]
        for n in range(poles):
            table = etab[n, :, lanes]
            for b in range(subs):
                sums[b] = sums[b] + table * carried[b, l, n : n + 1, :]
        for b in range(subs):
            rows = slice(b * SUB, (b + 1) * SUB)
            mixed = sums[b].astype(BF16).astype(F32) + skip_ref[:, lanes] * xs[rows, lanes]
            out_ref[rows, lanes] = (qs[rows, lanes] * mixed).astype(BF16)

    for copy in copies1 + copies2:
        copy.wait_send()
    for due, copy in edge_sends:

        @pl.when(due)
        def _():
            copy.wait_send()

    @pl.when(half == 0)
    def _():
        for o in range(MEMBERS):
            pltpu.make_async_remote_copy(
                tbuf.at[o], got1.at[0, member], sendx.at[o], recvx.at[member],
                device_id=place(1, group, o), device_id_type=MESH,
            ).wait_send()

    for o in range(1, MEMBERS):
        to = (member + o) % MEMBERS
        pltpu.make_async_remote_copy(
            cbuf.at[to], got3.at[member], send3.at[o], recv3.at[member],
            device_id=place(half, group, to), device_id_type=MESH,
        ).wait_send()


def per_device(
    query_stream, key_stream, value_stream, conv_weight, decay_rates, residues, skip_gain
):
    tokens, width = query_stream.shape
    poles = decay_rates.shape[0]
    z_len = lax.axis_size("ctx") // 2
    groups = z_len // MEMBERS
    quarters = width // LANES
    subs = tokens // SUB
    vmem = pltpu.VMEM
    state = (poles, LANES)
    message = (poles + EDGE, LANES)
    dma = pltpu.SemaphoreType.DMA
    whole = pl.BlockSpec(memory_space=pltpu.VMEM)
    outside = pl.BlockSpec(memory_space=pltpu.HBM)
    return pl.pallas_call(
        functools.partial(kernel, z_len, groups),
        out_shape=jax.ShapeDtypeStruct((tokens, width), BF16),
        in_specs=[outside] * 7,
        out_specs=whole,
        scratch_shapes=[
            vmem((3, 3, width), F32),
            vmem((poles, width), F32),
            vmem((poles, width), F32),
            vmem((1, width), F32),
            vmem((3, tokens, width), BF16),
            vmem((3, PAD + tokens, width), F32),
            vmem((8, width), F32),
            vmem((8, width), F32),
            vmem((tokens, width), F32),
            vmem((tokens, width), F32),
            vmem((poles, SUB, width), F32),
            vmem((2 * SUB, width), F32),
            vmem((SUB, SUB, width), F32),
            vmem((tokens, width), F32),
            vmem((subs, quarters) + state, F32),
            vmem((subs, quarters) + state, F32),
            vmem((4 + groups, quarters) + state, F32),
            vmem((quarters, 8, LANES), F32),
            vmem((quarters,) + state, F32),
            vmem((quarters,) + message, F32),
            vmem((2, MEMBERS) + message, F32),
            vmem((2, EDGE, LANES), F32),
            vmem((2,) + state, F32),
            vmem((groups,) + state, F32),
            vmem((MEMBERS,) + state, F32),
            vmem((quarters,) + state, F32),
            dma((7,)), pltpu.SemaphoreType.REGULAR, dma, dma,
            dma((MEMBERS,)), dma((MEMBERS,)), dma((MEMBERS,)), dma((MEMBERS,)),
            dma((MEMBERS,)), dma, dma((MEMBERS,)), dma,
            dma((groups,)), dma((groups,)), dma((MEMBERS,)), dma((MEMBERS,)),
        ],
        compiler_params=pltpu.CompilerParams(
            collective_id=0, has_side_effects=True, vmem_limit_bytes=40 * 1024 * 1024
        ),
        name="modal_scan",
    )(*[
        pltpu.with_memory_space_constraint(operand, pltpu.HBM)
        for operand in (query_stream, key_stream, value_stream, conv_weight, decay_rates,
                        residues, skip_gain.reshape(1, width))
    ])


def solution(mesh):
    in_specs = (
        P("ctx", "fsdp"),
        P("ctx", "fsdp"),
        P("ctx", "fsdp"),
        P(None, None, "fsdp"),
        P(None, "fsdp"),
        P(None, "fsdp"),
        P("fsdp"),
    )
    return jax.shard_map(
        per_device, mesh=mesh, in_specs=in_specs, out_specs=P("ctx", "fsdp"), check_vma=False
    )
```
